32 devices in a mesh: grp: 2 (over y), rcv: 16 (over z, x, core).
Axes of the slice: x: 2, y: 2, z: 4, core: 2. Of those that a mesh axis runs over, the one named last changes fastest.
Arguments:
- traces: bfloat16 [2, 3072, 5376], P(None, ('grp', 'rcv')), parts along dimension 1, may hold values from -17 to 17, as said below
- sketch: bfloat16 [2, 96, 5376], P(None, None, 'rcv'), may hold values from -0.0625 to 0.0625
Outputs:
- basis: float32 [2, 3072, 96], P(None, ('grp', 'rcv')), parts along dimension 1
- coeffs: float32 [2, 192, 5376], P(None, 'grp', 'rcv'), parts along dimension 1
The draws below stay inside these ranges and needn't reach their ends.
There are 2 independent parts, one for each index of `grp`. The reference program is written for one: setup_inputs(seed, part) draws one part's arguments, and reference() takes and returns one part's arrays. A program takes and returns all parts, laid end to end along the dimension named above; an argument that names none is the same for every part. Nothing has to cross between parts.
Inputs may be any that keep to these rules, and one draw needn't show every extreme that they name: `traces`: complex data, real part at index 0 and imaginary part at index 1 of the first dimension.
All inputs are finite; a program needn't handle non-finite values.
Results may differ from the reference program's by a relative error of at most 0.0015.
Values may be sent and summed in bfloat16 or wider, within the bound.
A program may use at most 64 MiB of HBM per device.

```python
import math
import jax
import jax.numpy as jnp
from jax import lax

SKETCH = 96
SOURCES = 5376
RECEIVERS = 1536


def draw_traces(key, part):
    first = jax.random.fold_in(key, 11)
    second = jax.random.fold_in(key, 12)
    third = jax.random.fold_in(key, 13)
    places = jnp.arange(RECEIVERS).astype(jnp.float32)
    trend = jnp.exp(-math.log(3.0) * places / max(RECEIVERS - 1, 1))
    base = jnp.clip(jax.random.normal(first, (2, RECEIVERS, SOURCES), jnp.float32), -5.0, 5.0)
    rough = jnp.exp(jax.random.uniform(second, (RECEIVERS,), jnp.float32, 0.0, math.log(3.3)))
    column = jnp.exp(jax.random.uniform(third, (SOURCES,), jnp.float32, math.log(0.5), math.log(2.0)))
    values = base * (trend * rough)[None, :, None] * column[None, None, :] * 0.5
    return values.astype(jnp.bfloat16)


def block_levels(key, extent, split, smallest, largest):
    loudness, own = 1.0, jax.random.fold_in(key, 6)
    for position, shards_of in split:
        heights = jnp.exp(jax.random.uniform(jax.random.fold_in(own, position), (shards_of,), jnp.float32, smallest / len(split), largest / len(split)))
        loudness = loudness * jnp.repeat(heights, extent[position] // shards_of).reshape([-1 if axis == position else 1 for axis in range(len(extent))])
    return loudness


def bell_draw(rng, extent, width, limit, split=(), held_as=jnp.bfloat16):
    drawn = jax.random.normal(rng, extent, jnp.float32) * width
    if len(split) > 0:
        drawn = block_levels(rng, extent, split, -0.22, 0.18) * drawn
    return jnp.clip(drawn, min=-limit, max=limit).astype(held_as)


def setup_inputs(seed: int = 0, part: int = 0) -> dict:
    arg_keys = jax.random.split(jax.random.key(seed), 3)
    own_keys = jax.random.split(jax.random.fold_in(arg_keys[2], part), 3)
    traces = draw_traces(jax.random.fold_in(jax.random.fold_in(arg_keys[2], part), 71), part)
    sketch = bell_draw(arg_keys[1], (2, SKETCH, SOURCES), (2 * SOURCES) ** -0.5, 0.0625, ((2, 16),))
    return dict(traces=traces, sketch=sketch)


def precise_dot(left, right):
    return jnp.dot(left.astype(jnp.float32), right.astype(jnp.float32), precision=lax.Precision.HIGHEST, preferred_element_type=jnp.float32)

def complex_product(left, right):
    return (precise_dot(left[0], right[0]) - precise_dot(left[1], right[1]), precise_dot(left[0], right[1]) + precise_dot(left[1], right[0]))

def adjoint(matrix):
    return (matrix[0].T, -matrix[1].T)

def factor(gram):
    count = gram[0].shape[0]
    embed = jnp.stack([jnp.stack([gram[0], -gram[1]], axis=-1), jnp.stack([gram[1], gram[0]], axis=-1)], axis=1)
    embed = embed.reshape(2 * count, 2 * count)
    lower = jnp.linalg.cholesky(embed)
    ident = jnp.eye(2 * count, dtype=jnp.float32)
    lower_inv = jax.scipy.linalg.solve_triangular(lower, ident, lower=True)
    low_re = lower[0::2, 0::2]
    low_im = lower[1::2, 0::2]
    linv_re = lower_inv[0::2, 0::2]
    linv_im = lower_inv[1::2, 0::2]
    return (low_re.T, -low_im.T, linv_re.T, -linv_im.T)

def reference(traces, sketch):
    data_re = traces[0]
    data_im = traces[1]
    sk_re = sketch[0].T
    sk_im = sketch[1].T
    sk_re_f = jnp.dot(data_re.astype(jnp.float32), sk_re.astype(jnp.float32), preferred_element_type=jnp.float32)
    sketched_re = sk_re_f - jnp.dot(data_im.astype(jnp.float32), sk_im.astype(jnp.float32), preferred_element_type=jnp.float32)
    sketched_im = jnp.dot(data_re.astype(jnp.float32), sk_im.astype(jnp.float32), preferred_element_type=jnp.float32) + jnp.dot(data_im.astype(jnp.float32), sk_re.astype(jnp.float32), preferred_element_type=jnp.float32)
    sketched = (sketched_re, sketched_im)
    gram = complex_product(adjoint(sketched), sketched)
    factors = factor(gram)
    ortho = complex_product(sketched, (factors[2], factors[3]))
    scale = math.sqrt(RECEIVERS)
    basis = jnp.stack([ortho[0] * scale, ortho[1] * scale])
    rounded_re = ortho[0].astype(jnp.bfloat16)
    rounded_im = ortho[1].astype(jnp.bfloat16)
    coef_re = jnp.dot(rounded_re.T.astype(jnp.float32), data_re.astype(jnp.float32), preferred_element_type=jnp.float32) + jnp.dot(rounded_im.T.astype(jnp.float32), data_im.astype(jnp.float32), preferred_element_type=jnp.float32)
    coef_im = jnp.dot(rounded_re.T.astype(jnp.float32), data_im.astype(jnp.float32), preferred_element_type=jnp.float32) - jnp.dot(rounded_im.T.astype(jnp.float32), data_re.astype(jnp.float32), preferred_element_type=jnp.float32)
    return (basis, jnp.stack([coef_re, coef_im]))
```

```python
import functools
import math

import jax
import jax.numpy as jnp
from jax import lax
from jax.experimental import pallas as pl
from jax.experimental.pallas import tpu as pltpu
from jax.sharding import PartitionSpec as P

VMEM = pltpu.VMEM
F32 = jnp.float32
BF16 = jnp.bfloat16
LIMIT = 67_000_000


def plan(n):
    chips = n // 2
    fast = max(d for d in range(1, chips + 1) if chips % d == 0 and d * d <= chips)
    return chips // fast, fast


def exact(left, right, dims):
    return lax.dot_general(
        left, right, (dims, ((), ())), precision=lax.Precision.HIGHEST, preferred_element_type=F32
    )


def remote(src, dst, send, recv, target):
    return pltpu.make_async_remote_copy(
        src_ref=src, dst_ref=dst, send_sem=send, recv_sem=recv,
        device_id={"rcv": target}, device_id_type=pl.DeviceIdType.MESH,
    )


def place(fast):
    me = lax.axis_index("rcv")
    chip = me // 2
    return me, chip // fast, chip % fast, me % 2


def greet(targets):
    barrier = pltpu.get_barrier_semaphore()
    for target in targets:
        pl.semaphore_signal(
            barrier, inc=1, device_id={"rcv": target}, device_id_type=pl.DeviceIdType.MESH
        )
    pl.semaphore_wait(barrier, len(targets))


def sketch_kernel(
    n, data, mine, sketched, gram_out,
    held, acc, own, pair_in, pair_sum, quick_in, line_in,
    up_send, down_send, side_send, core_send, recv,
    g_send, g_recv,
):
    slow, fast = plan(n)
    me, s, f, c = place(fast)
    half = sketched.shape[1]

    def index(a, b, e):
        return (a * fast + b) * 2 + e

    partner = index(s, f, 1 - c)
    sides = [index(s, (f + d) % fast, c) for d in range(1, fast)]
    lines = [index((s + d) % slow, f, c) for d in range(1, slow)]
    greet([partner] + sides + lines)

    def block(slot, first):
        return mine if first else held.at[slot]

    def to_up(slot, first=False):
        return remote(block(slot, first), held.at[slot], up_send.at[slot], recv.at[slot], index(jnp.minimum(s + 1, slow - 1), f, c))

    def to_down(slot, first=False):
        return remote(block(slot, first), held.at[slot], down_send.at[slot], recv.at[slot], index(jnp.maximum(s - 1, 0), f, c))

    def to_side(d, slot, first=False):
        return remote(block(slot, first), held.at[slot], side_send.at[d, slot], recv.at[slot], sides[d])

    def to_core(slot, first=False):
        return remote(block(slot, first), held.at[slot], core_send.at[slot], recv.at[slot], partner)

    def arrived(slot):
        remote(held.at[slot], held.at[slot], core_send.at[slot], recv.at[slot], partner).wait_recv()

    def add(slot, first=False):
        value = mine[...] if first else held[slot]
        acc[...] += lax.dot_general(
            data[slot], value, (((1,), (1,)), ((), ())), preferred_element_type=F32
        )

    pl.when(s < slow - 1)(lambda: to_up(me, True).start())
    pl.when(s > 0)(lambda: to_down(me, True).start())
    for d in range(fast - 1):
        to_side(d, me, True).start()
    to_core(me, True).start()
    acc[...] = jnp.zeros_like(acc)
    add(me, True)

    for d in range(1, slow):

        @pl.when(s - d >= 0)
        def _(d=d):
            slot = index(s - d, f, c)
            arrived(slot)
            pl.when(s < slow - 1)(lambda: to_up(slot).start())
            for e in range(fast - 1):
                to_side(e, slot).start()
            to_core(slot).start()
            add(slot)

        @pl.when(s + d < slow)
        def _(d=d):
            slot = index(s + d, f, c)
            arrived(slot)
            pl.when(s > 0)(lambda: to_down(slot).start())
            for e in range(fast - 1):
                to_side(e, slot).start()
            to_core(slot).start()
            add(slot)

    def across(b):
        for d in range(slow):
            for sign in ((1,) if d == 0 else (-1, 1)):

                @pl.when((s + sign * d >= 0) & (s + sign * d < slow))
                def _(d=d, sign=sign):
                    slot = index(s + sign * d, b, c)
                    arrived(slot)
                    to_core(slot).start()
                    add(slot)

    for d in range(1, fast):
        across((f + d) % fast)

    def other(b):
        for d in range(slow):
            for sign in ((1,) if d == 0 else (-1, 1)):

                @pl.when((s + sign * d >= 0) & (s + sign * d < slow))
                def _(d=d, sign=sign):
                    slot = index(s + sign * d, b, 1 - c)
                    arrived(slot)
                    add(slot)

    for d in range(fast):
        other((f + d) % fast)

    to_core(me, True).wait_send()
    pl.when(s < slow - 1)(lambda: to_up(me, True).wait_send())
    pl.when(s > 0)(lambda: to_down(me, True).wait_send())
    for e in range(fast - 1):
        to_side(e, me, True).wait_send()
    for d in range(1, slow):

        @pl.when(s - d >= 0)
        def _(d=d):
            slot = index(s - d, f, c)
            pl.when(s < slow - 1)(lambda: to_up(slot).wait_send())
            for e in range(fast - 1):
                to_side(e, slot).wait_send()
            to_core(slot).wait_send()

        @pl.when(s + d < slow)
        def _(d=d):
            slot = index(s + d, f, c)
            pl.when(s > 0)(lambda: to_down(slot).wait_send())
            for e in range(fast - 1):
                to_side(e, slot).wait_send()
            to_core(slot).wait_send()

    for d in range(1, fast):
        for a in range(slow):
            to_core(index(a, (f + d) % fast, c)).wait_send()

    rows = half
    width = sketched.shape[2]
    re = acc[:rows, :width] - acc[rows:, width:]
    im = acc[:rows, width:] + acc[rows:, :width]
    sketched[0] = re
    sketched[1] = im
    first = ((0,), (0,))
    gram_re = exact(re, re, first) + exact(im, im, first)
    gram_im = exact(re, im, first) - exact(im, re, first)
    row = lax.broadcasted_iota(jnp.int32, gram_re.shape, 0)
    col = lax.broadcasted_iota(jnp.int32, gram_re.shape, 1)
    own[...] = jnp.where(col >= row, gram_re, gram_im)

    step = remote(own, pair_in, g_send.at[0], g_recv.at[0], partner)
    step.start()
    step.wait()
    pair_sum[...] = own[...] + pair_in[...]
    steps = [
        remote(pair_sum, quick_in.at[d], g_send.at[1 + d], g_recv.at[1 + d], sides[d])
        for d in range(fast - 1)
    ]
    for step in steps:
        step.start()
    for step in steps:
        step.wait()
    total = pair_sum[...]
    for d in range(fast - 1):
        total = total + quick_in[d]
    line_in[s] = total
    steps = [
        remote(line_in.at[s], line_in.at[s], g_send.at[fast + d], g_recv.at[fast + d], lines[d])
        for d in range(slow - 1)
    ]
    for step in steps:
        step.start()
    for d in range(slow - 1):
        steps[d].wait()
    total = line_in[0]
    for a in range(1, slow):
        total = total + line_in[a]
    gram_out[...] = total


def factor_kernel(scale, gram, sketched, basis, weights):
    packed = gram[...]
    width = packed.shape[0]
    turned = packed.T
    row = lax.broadcasted_iota(jnp.int32, packed.shape, 0)
    col = lax.broadcasted_iota(jnp.int32, packed.shape, 1)
    g_re = jnp.where(col >= row, packed, turned)
    g_im = jnp.where(row > col, packed, jnp.where(row < col, -turned, 0.0))
    tile = 8
    count = width // tile
    re = [g_re[tile * i : tile * (i + 1)] for i in range(count)]
    im = [g_im[tile * i : tile * (i + 1)] for i in range(count)]
    lane = lax.broadcasted_iota(jnp.int32, (tile, width), 1)
    sub = lax.broadcasted_iota(jnp.int32, (tile, width), 0)
    for k in range(width):
        at, inside = divmod(k, tile)
        d = re[at][inside : inside + 1, k : k + 1]
        here = lane[:1] == k
        p_re = jnp.where(here, 1.0, re[at][inside : inside + 1, :])
        p_im = jnp.where(here, 0.0, im[at][inside : inside + 1, :])
        inv = 1.0 / d
        q_re = p_re * inv
        q_im = p_im * inv
        for i in range(at, count):
            c_re = re[i][:, k : k + 1]
            c_im = im[i][:, k : k + 1]
            old_re = jnp.where(lane == k, 0.0, re[i])
            old_im = jnp.where(lane == k, 0.0, im[i])
            new_re = old_re - (c_re * q_re - c_im * q_im)
            new_im = old_im - (c_re * q_im + c_im * q_re)
            if i == at:
                root = lax.rsqrt(d)
                new_re = jnp.where(sub > inside, new_re, jnp.where(sub == inside, jnp.where(lane > k, 0.0, p_re * root), re[i]))
                new_im = jnp.where(sub > inside, new_im, jnp.where(sub == inside, jnp.where(lane > k, 0.0, p_im * root), im[i]))
            re[i] = new_re
            im[i] = new_im
    l_re = jnp.concatenate(re, axis=0)
    l_im = jnp.concatenate(im, axis=0)
    s_re, s_im = sketched[0], sketched[1]
    last = ((1,), (1,))
    o_re = exact(s_re, l_re, last) + exact(s_im, l_im, last)
    o_im = exact(s_im, l_re, last) - exact(s_re, l_im, last)
    basis[0] = o_re * scale
    basis[1] = o_im * scale
    t_re, t_im = o_re.T, o_im.T
    rows = o_re.shape[0]
    weights[:width, :rows] = t_re.astype(BF16)
    weights[:width, rows:] = t_im.astype(BF16)
    weights[width:, :rows] = (-t_im).astype(BF16)
    weights[width:, rows:] = t_re.astype(BF16)


def project_kernel(
    n, data, weights, out,
    kept, away, from_core, side_out, side_in, line_out, line_in,
    c_send, c_recv, s_send, s_recv, u_send, u_recv, d_send, d_recv,
):
    slow, fast = plan(n)
    me, s, f, c = place(fast)

    def index(a, b, e):
        return (a * fast + b) * 2 + e

    partner = index(s, f, 1 - c)
    sides = [index(s, (f + d) % fast, c) for d in range(1, fast)]
    lines = [index((s + d) % slow, f, c) for d in range(1, slow)]
    greet([partner] + sides + lines)

    def product(slot):
        return jnp.dot(weights[...], data[slot], preferred_element_type=F32)

    def core_copy(t, d):
        return remote(away.at[d, t], from_core.at[d, t], c_send.at[d, t], c_recv.at[d, t], partner)

    def side_copy(t, d):
        return remote(side_out.at[d, t], side_in.at[d, t], s_send.at[d, t], s_recv.at[d, t], sides[d - 1])

    low = s < slow - s - 1

    def target(t):
        return jnp.where(low, slow - 1 - t, t)

    def begin(t, d):
        a, b = target(t), (f + d) % fast
        away[d, t] = product(index(a, b, 1 - c))
        core_copy(t, d).start()
        kept[d, t] = product(index(a, b, c))

    def middle(t, d):
        core_copy(t, d).wait()
        value = kept[d, t] + from_core[d, t]
        if d == 0:
            kept[0, t] = value
        else:
            side_out[d, t] = value.astype(BF16)
            side_copy(t, d).start()

    order = [(t, d) for t in range(slow) for d in list(range(1, fast)) + [0]]

    def up_copy(a):
        return remote(line_out.at[a], line_in.at[a], u_send.at[a], u_recv.at[a], index(jnp.minimum(s + 1, slow - 1), f, c))

    def down_copy(a):
        slot = jnp.where(a == s - 1, slow, a)
        return remote(line_out.at[a], line_in.at[slot], d_send.at[a], d_recv.at[a], index(jnp.maximum(s - 1, 0), f, c))

    def finish(t):
        a = target(t)
        for d in range(1, fast):
            side_copy(t, d).wait()
        value = kept[0, t]
        for d in range(1, fast):
            value = value + side_in[d, t].astype(F32)
        kept[0, t] = value

        @pl.when(a > s)
        def _():
            @pl.when(s > 0)
            def _():
                up_copy(a).wait_recv()
                line_out[a] = kept[0, t] + line_in[a]

            @pl.when(s == 0)
            def _():
                line_out[a] = kept[0, t]

            up_copy(a).start()

        @pl.when(a < s)
        def _():
            @pl.when(s < slow - 1)
            def _():
                down_copy(a).wait_recv()
                line_out[a] = kept[0, t] + line_in[a]

            @pl.when(s == slow - 1)
            def _():
                line_out[a] = kept[0, t]

            down_copy(a).start()

        @pl.when(a == s)
        def _():
            out[...] = kept[0, t]

    for i, pair in enumerate(order):
        begin(*pair)
        if i:
            middle(*order[i - 1])
    middle(*order[-1])
    for t in range(slow):
        finish(t)

    @pl.when(s > 0)
    def _():
        up_copy(s).wait_recv()
        out[...] += line_in[s]

    @pl.when(s < slow - 1)
    def _():
        down_copy(s).wait_recv()
        out[...] += line_in[slow]

    for a in range(slow):
        pl.when(a > s)(lambda a=a: up_copy(a).wait_send())
        pl.when(a < s)(lambda a=a: down_copy(a).wait_send())


def per_device(n, traces, sketch):
    slow, fast = plan(n)
    parts, rows, sources = traces.shape
    width, share = sketch.shape[1], sketch.shape[2]
    data = traces.reshape(parts * rows, n, share).transpose(1, 0, 2)
    mine = sketch.reshape(parts * width, share)
    dma = pltpu.SemaphoreType.DMA
    vmem = pl.BlockSpec(memory_space=VMEM)
    two = 2 * width
    sketched, gram = pl.pallas_call(
        functools.partial(sketch_kernel, n),
        out_shape=(
            jax.ShapeDtypeStruct((2, rows, width), F32),
            jax.ShapeDtypeStruct((width, width), F32),
        ),
        in_specs=[vmem] * 2,
        out_specs=(vmem, vmem),
        scratch_shapes=[
            VMEM((n, two, share), BF16),
            VMEM((2 * rows, two), F32),
            VMEM((width, width), F32),
            VMEM((width, width), F32),
            VMEM((width, width), F32),
            VMEM((max(fast - 1, 1), width, width), F32),
            VMEM((slow, width, width), F32),
            dma((n,)),
            dma((n,)),
            dma((max(fast - 1, 1), n)),
            dma((n,)),
            dma((n,)),
            dma((slow + fast,)),
            dma((slow + fast,)),
        ],
        compiler_params=pltpu.CompilerParams(
            collective_id=0, has_side_effects=True, vmem_limit_bytes=LIMIT
        ),
        name="gather_sketch",
    )(data, mine)
    scale = math.sqrt(rows * n)
    basis, weights = pl.pallas_call(
        functools.partial(factor_kernel, scale),
        out_shape=(
            jax.ShapeDtypeStruct((2, rows, width), F32),
            jax.ShapeDtypeStruct((two, 2 * rows), BF16),
        ),
        in_specs=[vmem] * 2,
        out_specs=(vmem, vmem),
        compiler_params=pltpu.CompilerParams(vmem_limit_bytes=LIMIT),
        name="factor",
    )(gram, sketched)
    chunk = (two, share)
    coeffs = pl.pallas_call(
        functools.partial(project_kernel, n),
        out_shape=jax.ShapeDtypeStruct(chunk, F32),
        in_specs=[vmem] * 2,
        out_specs=vmem,
        scratch_shapes=[
            VMEM((fast, slow) + chunk, F32),
            VMEM((fast, slow) + chunk, F32),
            VMEM((fast, slow) + chunk, F32),
            VMEM((fast, slow) + chunk, BF16),
            VMEM((fast, slow) + chunk, BF16),
            VMEM((slow,) + chunk, F32),
            VMEM((slow + 1,) + chunk, F32),
            dma((fast, slow)),
            dma((fast, slow)),
            dma((fast, slow)),
            dma((fast, slow)),
            dma((slow,)),
            dma((slow,)),
            dma((slow,)),
            dma((slow,)),
        ],
        compiler_params=pltpu.CompilerParams(
            collective_id=1, has_side_effects=True, vmem_limit_bytes=LIMIT
        ),
        name="project",
    )(data, weights)
    return basis, coeffs.reshape(2, width, share)


def solution(mesh):
    return jax.shard_map(
        functools.partial(per_device, mesh.shape["rcv"]),
        mesh=mesh,
        in_specs=(P(None, ("grp", "rcv"), None), P(None, None, "rcv")),
        out_specs=(P(None, ("grp", "rcv"), None), P(None, "grp", "rcv")),
        check_vma=False,
    )
```

```python
import functools
import math

import jax
import jax.numpy as jnp
from jax import lax
from jax.experimental import pallas as pl
from jax.experimental.pallas import tpu as pltpu
from jax.sharding import PartitionSpec as P

VMEM = pltpu.VMEM
F32 = jnp.float32
BF16 = jnp.bfloat16
LIMIT = 67_000_000


def plan(n):
    chips = n // 2
    fast = max(d for d in range(1, chips + 1) if chips % d == 0 and d * d <= chips)
    return chips // fast, fast


def exact(left, right, dims):
    return lax.dot_general(
        left, right, (dims, ((), ())), precision=lax.Precision.HIGHEST, preferred_element_type=F32
    )


def remote(src, dst, send, recv, target):
    return pltpu.make_async_remote_copy(
        src_ref=src, dst_ref=dst, send_sem=send, recv_sem=recv,
        device_id={"rcv": target}, device_id_type=pl.DeviceIdType.MESH,
    )


def place(fast):
    me = lax.axis_index("rcv")
    chip = me // 2
    return me, chip // fast, chip % fast, me % 2


def greet(targets):
    barrier = pltpu.get_barrier_semaphore()
    for target in targets:
        pl.semaphore_signal(
            barrier, inc=1, device_id={"rcv": target}, device_id_type=pl.DeviceIdType.MESH
        )
    pl.semaphore_wait(barrier, len(targets))


def sketch_kernel(
    n, data, mine, sketched, gram_out,
    held, acc, own, pair_in, pair_sum, quick_in, line_in,
    up_send, down_send, side_send, core_send, recv,
    g_send, g_recv,
):
    slow, fast = plan(n)
    me, s, f, c = place(fast)
    half = sketched.shape[1]

    def index(a, b, e):
        return (a * fast + b) * 2 + e

    partner = index(s, f, 1 - c)
    sides = [index(s, (f + d) % fast, c) for d in range(1, fast)]
    lines = [index((s + d) % slow, f, c) for d in range(1, slow)]
    greet([partner] + sides + lines)

    def block(slot, first):
        return mine if first else held.at[slot]

    def to_up(slot, first=False):
        return remote(block(slot, first), held.at[slot], up_send.at[slot], recv.at[slot], index(jnp.minimum(s + 1, slow - 1), f, c))

    def to_down(slot, first=False):
        return remote(block(slot, first), held.at[slot], down_send.at[slot], recv.at[slot], index(jnp.maximum(s - 1, 0), f, c))

    def to_side(d, slot, first=False):
        return remote(block(slot, first), held.at[slot], side_send.at[d, slot], recv.at[slot], sides[d])

    def to_core(slot, first=False):
        return remote(block(slot, first), held.at[slot], core_send.at[slot], recv.at[slot], partner)

    def arrived(slot):
        remote(held.at[slot], held.at[slot], core_send.at[slot], recv.at[slot], partner).wait_recv()

    def add(slot, first=False):
        value = mine[...] if first else held[slot]
        acc[...] += lax.dot_general(
            data[slot], value, (((1,), (1,)), ((), ())), preferred_element_type=F32
        )

    pl.when(s < slow - 1)(lambda: to_up(me, True).start())
    pl.when(s > 0)(lambda: to_down(me, True).start())
    for d in range(fast - 1):
        to_side(d, me, True).start()
    to_core(me, True).start()
    acc[...] = jnp.zeros_like(acc)
    add(me, True)

    for d in range(1, slow):

        @pl.when(s - d >= 0)
        def _(d=d):
            slot = index(s - d, f, c)
            arrived(slot)
            pl.when(s < slow - 1)(lambda: to_up(slot).start())
            for e in range(fast - 1):
                to_side(e, slot).start()
            to_core(slot).start()
            add(slot)

        @pl.when(s + d < slow)
        def _(d=d):
            slot = index(s + d, f, c)
            arrived(slot)
            pl.when(s > 0)(lambda: to_down(slot).start())
            for e in range(fast - 1):
                to_side(e, slot).start()
            to_core(slot).start()
            add(slot)

    def across(b):
        for d in range(slow):
            for sign in ((1,) if d == 0 else (-1, 1)):

                @pl.when((s + sign * d >= 0) & (s + sign * d < slow))
                def _(d=d, sign=sign):
                    slot = index(s + sign * d, b, c)
                    arrived(slot)
                    to_core(slot).start()
                    add(slot)

    for d in range(1, fast):
        across((f + d) % fast)

    def other(b):
        for d in range(slow):
            for sign in ((1,) if d == 0 else (-1, 1)):

                @pl.when((s + sign * d >= 0) & (s + sign * d < slow))
                def _(d=d, sign=sign):
                    slot = index(s + sign * d, b, 1 - c)
                    arrived(slot)
                    add(slot)

    for d in range(fast):
        other((f + d) % fast)

    to_core(me, True).wait_send()
    pl.when(s < slow - 1)(lambda: to_up(me, True).wait_send())
    pl.when(s > 0)(lambda: to_down(me, True).wait_send())
    for e in range(fast - 1):
        to_side(e, me, True).wait_send()
    for d in range(1, slow):

        @pl.when(s - d >= 0)
        def _(d=d):
            slot = index(s - d, f, c)
            pl.when(s < slow - 1)(lambda: to_up(slot).wait_send())
            for e in range(fast - 1):
                to_side(e, slot).wait_send()
            to_core(slot).wait_send()

        @pl.when(s + d < slow)
        def _(d=d):
            slot = index(s + d, f, c)
            pl.when(s > 0)(lambda: to_down(slot).wait_send())
            for e in range(fast - 1):
                to_side(e, slot).wait_send()
            to_core(slot).wait_send()

    for d in range(1, fast):
        for a in range(slow):
            to_core(index(a, (f + d) % fast, c)).wait_send()

    rows = half
    width = sketched.shape[2]
    re = acc[:rows, :width] - acc[rows:, width:]
    im = acc[:rows, width:] + acc[rows:, :width]
    sketched[0] = re
    sketched[1] = im
    first = ((0,), (0,))
    gram_re = exact(re, re, first) + exact(im, im, first)
    gram_im = exact(re, im, first) - exact(im, re, first)
    row = lax.broadcasted_iota(jnp.int32, gram_re.shape, 0)
    col = lax.broadcasted_iota(jnp.int32, gram_re.shape, 1)
    own[...] = jnp.where(col >= row, gram_re, gram_im)

    step = remote(own, pair_in, g_send.at[0], g_recv.at[0], partner)
    step.start()
    step.wait()
    pair_sum[...] = own[...] + pair_in[...]
    steps = [
        remote(pair_sum, quick_in.at[d], g_send.at[1 + d], g_recv.at[1 + d], sides[d])
        for d in range(fast - 1)
    ]
    for step in steps:
        step.start()
    for step in steps:
        step.wait()
    total = pair_sum[...]
    for d in range(fast - 1):
        total = total + quick_in[d]
    line_in[s] = total
    steps = [
        remote(line_in.at[s], line_in.at[s], g_send.at[fast + d], g_recv.at[fast + d], lines[d])
        for d in range(slow - 1)
    ]
    for step in steps:
        step.start()
    for d in range(slow - 1):
        steps[d].wait()
    total = line_in[0]
    for a in range(1, slow):
        total = total + line_in[a]
    gram_out[...] = total


def factor_kernel(scale, gram, sketched, basis, weights):
    packed = gram[...]
    width = packed.shape[0]
    turned = packed.T
    row = lax.broadcasted_iota(jnp.int32, packed.shape, 0)
    col = lax.broadcasted_iota(jnp.int32, packed.shape, 1)
    g_re = jnp.where(col >= row, packed, turned)
    g_im = jnp.where(row > col, packed, jnp.where(row < col, -turned, 0.0))
    tile = 8
    count = width // tile
    re = [g_re[tile * i : tile * (i + 1)] for i in range(count)]
    im = [g_im[tile * i : tile * (i + 1)] for i in range(count)]
    lane = lax.broadcasted_iota(jnp.int32, (tile, width), 1)
    sub = lax.broadcasted_iota(jnp.int32, (tile, width), 0)
    for k in range(width):
        at, inside = divmod(k, tile)
        d = re[at][inside : inside + 1, k : k + 1]
        here = lane[:1] == k
        p_re = jnp.where(here, 1.0, re[at][inside : inside + 1, :])
        p_im = jnp.where(here, 0.0, im[at][inside : inside + 1, :])
        inv = 1.0 / d
        q_re = p_re * inv
        q_im = p_im * inv
        for i in range(at, count):
            c_re = re[i][:, k : k + 1]
            c_im = im[i][:, k : k + 1]
            old_re = jnp.where(lane == k, 0.0, re[i])
            old_im = jnp.where(lane == k, 0.0, im[i])
            new_re = old_re - (c_re * q_re - c_im * q_im)
            new_im = old_im - (c_re * q_im + c_im * q_re)
            if i == at:
                root = lax.rsqrt(d)
                new_re = jnp.where(sub > inside, new_re, jnp.where(sub == inside, jnp.where(lane > k, 0.0, p_re * root), re[i]))
                new_im = jnp.where(sub > inside, new_im, jnp.where(sub == inside, jnp.where(lane > k, 0.0, p_im * root), im[i]))
            re[i] = new_re
            im[i] = new_im
    l_re = jnp.concatenate(re, axis=0)
    l_im = jnp.concatenate(im, axis=0)
    s_re, s_im = sketched[0], sketched[1]
    last = ((1,), (1,))
    o_re = exact(s_re, l_re, last) + exact(s_im, l_im, last)
    o_im = exact(s_im, l_re, last) - exact(s_re, l_im, last)
    basis[0] = o_re * scale
    basis[1] = o_im * scale
    t_re, t_im = o_re.T, o_im.T
    rows = o_re.shape[0]
    weights[:width, :rows] = t_re.astype(BF16)
    weights[:width, rows:] = t_im.astype(BF16)
    weights[width:, :rows] = (-t_im).astype(BF16)
    weights[width:, rows:] = t_re.astype(BF16)


def project_kernel(
    n, pieces, data, weights, out,
    kept, away, from_core, side_out, side_in, line_out, line_in,
    c_send, c_recv, s_send, s_recv, u_send, u_recv, d_send, d_recv,
):
    slow, fast = plan(n)
    me, s, f, c = place(fast)
    depth = out.shape[0] // pieces

    def index(a, b, e):
        return (a * fast + b) * 2 + e

    partner = index(s, f, 1 - c)
    sides = [index(s, (f + d) % fast, c) for d in range(1, fast)]
    lines = [index((s + d) % slow, f, c) for d in range(1, slow)]
    greet([partner] + sides + lines)

    def rows(p):
        return pl.ds(p * depth, depth)

    def product(slot):
        return jnp.dot(weights[...], data[slot], preferred_element_type=F32)

    def core_copy(t, d, p):
        return remote(away.at[d, t, rows(p)], from_core.at[d, t, rows(p)], c_send.at[d, t, p], c_recv.at[d, t, p], partner)

    def side_copy(t, d, p):
        return remote(side_out.at[d, t, rows(p)], side_in.at[d, t, rows(p)], s_send.at[d, t, p], s_recv.at[d, t, p], sides[d - 1])

    orders = [
        sorted(range(slow), key=lambda a: (-abs(a - b), -a if 2 * b < slow else a)) for b in range(slow)
    ]

    def target(t):
        value = 0
        for b in range(slow):
            value = value + jnp.where(s == b, orders[b][t], 0)
        return value

    owners = [target(t) for t in range(slow)]

    def begin(t, d):
        a, b = owners[t], (f + d) % fast
        away[d, t] = product(index(a, b, 1 - c))
        for p in range(pieces):
            core_copy(t, d, p).start()
        kept[d, t] = product(index(a, b, c))

    def middle(t, d):
        for p in range(pieces):
            core_copy(t, d, p).wait()
            value = kept[d, t, rows(p)] + from_core[d, t, rows(p)]
            if d == 0:
                kept[0, t, rows(p)] = value
            else:
                side_out[d, t, rows(p)] = value.astype(BF16)
                side_copy(t, d, p).start()

    order = [(t, d) for t in range(slow) for d in list(range(1, fast)) + [0]]

    def up_copy(a, p):
        return remote(line_out.at[a, rows(p)], line_in.at[a, rows(p)], u_send.at[a, p], u_recv.at[a, p], index(jnp.minimum(s + 1, slow - 1), f, c))

    def down_copy(a, p):
        slot = jnp.where(a == s - 1, slow, a)
        return remote(line_out.at[a, rows(p)], line_in.at[slot, rows(p)], d_send.at[a, p], d_recv.at[a, p], index(jnp.maximum(s - 1, 0), f, c))

    def finish(t):
        a = owners[t]
        for p in range(pieces):
            for d in range(1, fast):
                side_copy(t, d, p).wait()
            value = kept[0, t, rows(p)]
            for d in range(1, fast):
                value = value + side_in[d, t, rows(p)].astype(F32)

            if t == slow - 1:
                out[rows(p)] = value
                continue
            kept[0, t, rows(p)] = value

            @pl.when(a > s)
            def _():
                @pl.when(s > 0)
                def _():
                    up_copy(a, p).wait_recv()
                    line_out[a, rows(p)] = kept[0, t, rows(p)] + line_in[a, rows(p)]

                @pl.when(s == 0)
                def _():
                    line_out[a, rows(p)] = kept[0, t, rows(p)]

                up_copy(a, p).start()

            @pl.when(a < s)
            def _():
                @pl.when(s < slow - 1)
                def _():
                    down_copy(a, p).wait_recv()
                    line_out[a, rows(p)] = kept[0, t, rows(p)] + line_in[a, rows(p)]

                @pl.when(s == slow - 1)
                def _():
                    line_out[a, rows(p)] = kept[0, t, rows(p)]

                down_copy(a, p).start()

    def settle(i):
        middle(*order[i])
        t, d = order[i]
        if d == 0 and t > 0:
            finish(t - 1)

    for i, pair in enumerate(order):
        begin(*pair)
        if i:
            settle(i - 1)
    settle(len(order) - 1)
    finish(slow - 1)

    for p in range(pieces):

        @pl.when(s > 0)
        def _():
            up_copy(s, p).wait_recv()
            out[rows(p)] += line_in[s, rows(p)]

        @pl.when(s < slow - 1)
        def _():
            down_copy(s, p).wait_recv()
            out[rows(p)] += line_in[slow, rows(p)]

    for t in range(slow - 1):
        a = owners[t]
        for p in range(pieces):
            pl.when(a > s)(lambda: up_copy(a, p).wait_send())
            pl.when(a < s)(lambda: down_copy(a, p).wait_send())


def per_device(n, traces, sketch):
    slow, fast = plan(n)
    parts, rows, sources = traces.shape
    width, share = sketch.shape[1], sketch.shape[2]
    data = traces.reshape(parts * rows, n, share).transpose(1, 0, 2)
    mine = sketch.reshape(parts * width, share)
    dma = pltpu.SemaphoreType.DMA
    vmem = pl.BlockSpec(memory_space=VMEM)
    two = 2 * width
    sketched, gram = pl.pallas_call(
        functools.partial(sketch_kernel, n),
        out_shape=(
            jax.ShapeDtypeStruct((2, rows, width), F32),
            jax.ShapeDtypeStruct((width, width), F32),
        ),
        in_specs=[vmem] * 2,
        out_specs=(vmem, vmem),
        scratch_shapes=[
            VMEM((n, two, share), BF16),
            VMEM((2 * rows, two), F32),
            VMEM((width, width), F32),
            VMEM((width, width), F32),
            VMEM((width, width), F32),
            VMEM((max(fast - 1, 1), width, width), F32),
            VMEM((slow, width, width), F32),
            dma((n,)),
            dma((n,)),
            dma((max(fast - 1, 1), n)),
            dma((n,)),
            dma((n,)),
            dma((slow + fast,)),
            dma((slow + fast,)),
        ],
        compiler_params=pltpu.CompilerParams(
            collective_id=0, has_side_effects=True, vmem_limit_bytes=LIMIT
        ),
        name="gather_sketch",
    )(data, mine)
    scale = math.sqrt(rows * n)
    basis, weights = pl.pallas_call(
        functools.partial(factor_kernel, scale),
        out_shape=(
            jax.ShapeDtypeStruct((2, rows, width), F32),
            jax.ShapeDtypeStruct((two, 2 * rows), BF16),
        ),
        in_specs=[vmem] * 2,
        out_specs=(vmem, vmem),
        compiler_params=pltpu.CompilerParams(vmem_limit_bytes=LIMIT),
        name="factor",
    )(gram, sketched)
    chunk = (two, share)
    pieces = 4 if n <= 64 and two % 64 == 0 else 1
    coeffs = pl.pallas_call(
        functools.partial(project_kernel, n, pieces),
        out_shape=jax.ShapeDtypeStruct(chunk, F32),
        in_specs=[vmem] * 2,
        out_specs=vmem,
        scratch_shapes=[
            VMEM((fast, slow) + chunk, F32),
            VMEM((fast, slow) + chunk, F32),
            VMEM((fast, slow) + chunk, F32),
            VMEM((fast, slow) + chunk, BF16),
            VMEM((fast, slow) + chunk, BF16),
            VMEM((slow,) + chunk, F32),
            VMEM((slow + 1,) + chunk, F32),
            dma((fast, slow, pieces)),
            dma((fast, slow, pieces)),
            dma((fast, slow, pieces)),
            dma((fast, slow, pieces)),
            dma((slow, pieces)),
            dma((slow, pieces)),
            dma((slow, pieces)),
            dma((slow, pieces)),
        ],
        compiler_params=pltpu.CompilerParams(
            collective_id=1, has_side_effects=True, vmem_limit_bytes=LIMIT
        ),
        name="project",
    )(data, weights)
    return basis, coeffs.reshape(2, width, share)


def solution(mesh):
    return jax.shard_map(
        functools.partial(per_device, mesh.shape["rcv"]),
        mesh=mesh,
        in_specs=(P(None, ("grp", "rcv"), None), P(None, None, "rcv")),
        out_specs=(P(None, ("grp", "rcv"), None), P(None, "grp", "rcv")),
        check_vma=False,
    )
```

```python
import functools
import math

import jax
import jax.numpy as jnp
from jax import lax
from jax.experimental import pallas as pl
from jax.experimental.pallas import tpu as pltpu
from jax.sharding import PartitionSpec as P

VMEM = pltpu.VMEM
F32 = jnp.float32
BF16 = jnp.bfloat16
LIMIT = 67_000_000


def plan(n):
    chips = n // 2
    fast = max(d for d in range(1, chips + 1) if chips % d == 0 and d * d <= chips)
    return chips // fast, fast


def exact(left, right, dims):
    return lax.dot_general(
        left, right, (dims, ((), ())), precision=lax.Precision.HIGHEST, preferred_element_type=F32
    )


def remote(src, dst, send, recv, target):
    return pltpu.make_async_remote_copy(
        src_ref=src, dst_ref=dst, send_sem=send, recv_sem=recv,
        device_id={"rcv": target}, device_id_type=pl.DeviceIdType.MESH,
    )


def place(fast):
    me = lax.axis_index("rcv")
    chip = me // 2
    return me, chip // fast, chip % fast, me % 2


def greet(targets):
    barrier = pltpu.get_barrier_semaphore()
    for target in targets:
        pl.semaphore_signal(
            barrier, inc=1, device_id={"rcv": target}, device_id_type=pl.DeviceIdType.MESH
        )
    pl.semaphore_wait(barrier, len(targets))


def factor(scale, gram, sketched, basis, weights):
    packed = gram[...]
    width = packed.shape[0]
    turned = packed.T
    row = lax.broadcasted_iota(jnp.int32, packed.shape, 0)
    col = lax.broadcasted_iota(jnp.int32, packed.shape, 1)
    g_re = jnp.where(col >= row, packed, turned)
    g_im = jnp.where(row > col, packed, jnp.where(row < col, -turned, 0.0))
    tile = 8
    count = width // tile
    re = [g_re[tile * i : tile * (i + 1)] for i in range(count)]
    im = [g_im[tile * i : tile * (i + 1)] for i in range(count)]
    lane = lax.broadcasted_iota(jnp.int32, (tile, width), 1)
    sub = lax.broadcasted_iota(jnp.int32, (tile, width), 0)
    for k in range(width):
        at, inside = divmod(k, tile)
        d = re[at][inside : inside + 1, k : k + 1]
        here = lane[:1] == k
        p_re = jnp.where(here, 1.0, re[at][inside : inside + 1, :])
        p_im = jnp.where(here, 0.0, im[at][inside : inside + 1, :])
        inv = 1.0 / d
        q_re = p_re * inv
        q_im = p_im * inv
        for i in range(at, count):
            c_re = re[i][:, k : k + 1]
            c_im = im[i][:, k : k + 1]
            old_re = jnp.where(lane == k, 0.0, re[i])
            old_im = jnp.where(lane == k, 0.0, im[i])
            new_re = old_re - (c_re * q_re - c_im * q_im)
            new_im = old_im - (c_re * q_im + c_im * q_re)
            if i == at:
                root = lax.rsqrt(d)
                new_re = jnp.where(sub > inside, new_re, jnp.where(sub == inside, jnp.where(lane > k, 0.0, p_re * root), re[i]))
                new_im = jnp.where(sub > inside, new_im, jnp.where(sub == inside, jnp.where(lane > k, 0.0, p_im * root), im[i]))
            re[i] = new_re
            im[i] = new_im
    l_re = jnp.concatenate(re, axis=0)
    l_im = jnp.concatenate(im, axis=0)
    s_re, s_im = sketched[0], sketched[1]
    last = ((1,), (1,))
    o_re = exact(s_re, l_re, last) + exact(s_im, l_im, last)
    o_im = exact(s_im, l_re, last) - exact(s_re, l_im, last)
    basis[0] = o_re * scale
    basis[1] = o_im * scale
    t_re, t_im = o_re.T, o_im.T
    rows = o_re.shape[0]
    weights[:width, :rows] = t_re.astype(BF16)
    weights[:width, rows:] = t_im.astype(BF16)
    weights[width:, :rows] = (-t_im).astype(BF16)
    weights[width:, rows:] = t_re.astype(BF16)


def project(
    n, pieces, data, weights, out, held,
    kept, fresh, away, from_core, line_out, line_in,
    c_send, c_recv, s_send, s_recv, u_send, u_recv, d_send, d_recv,
):
    slow, fast = plan(n)
    me, s, f, c = place(fast)
    depth = out.shape[0] // pieces

    def index(a, b, e):
        return (a * fast + b) * 2 + e

    partner = index(s, f, 1 - c)
    sides = [index(s, (f + d) % fast, c) for d in range(1, fast)]

    def rows(p):
        return pl.ds(p * depth, depth)

    def product(slot):
        return jnp.dot(weights[...], data[slot], preferred_element_type=F32)

    def core_copy(t, d, p):
        return remote(away.at[d, t, rows(p)], from_core.at[d, t, rows(p)], c_send.at[d, t, p], c_recv.at[d, t, p], partner)

    def side_copy(t, d, p):
        return remote(held.at[d * slow + t, rows(p)], held.at[n // 2 + d * slow + t, rows(p)], s_send.at[d, t, p], s_recv.at[d, t, p], sides[d - 1])

    orders = [
        sorted(range(slow), key=lambda a: (-abs(a - b), -a if 2 * b < slow else a)) for b in range(slow)
    ]

    def target(t):
        value = 0
        for b in range(slow):
            value = value + jnp.where(s == b, orders[b][t], 0)
        return value

    owners = [target(t) for t in range(slow)]

    def begin(t, d):
        a, b = owners[t], (f + d) % fast
        away[d, t] = product(index(a, b, 1 - c))
        for p in range(pieces):
            core_copy(t, d, p).start()

    def middle(t, d):
        into = kept.at[t] if d == 0 else fresh
        into[...] = product(index(owners[t], (f + d) % fast, c))
        for p in range(pieces):
            core_copy(t, d, p).wait()
            value = into[rows(p)] + from_core[d, t, rows(p)]
            if d == 0:
                kept[t, rows(p)] = value
            else:
                held[d * slow + t, rows(p)] = value.astype(BF16)
                side_copy(t, d, p).start()

    order = [(t, d) for t in range(slow) for d in list(range(1, fast)) + [0]]

    def up_copy(a, p):
        return remote(line_out.at[a, rows(p)], line_in.at[a, rows(p)], u_send.at[a, p], u_recv.at[a, p], index(jnp.minimum(s + 1, slow - 1), f, c))

    def down_copy(a, p):
        slot = jnp.where(a == s - 1, slow, a)
        return remote(line_out.at[a, rows(p)], line_in.at[slot, rows(p)], d_send.at[a, p], d_recv.at[a, p], index(jnp.maximum(s - 1, 0), f, c))

    def finish(t):
        a = owners[t]
        for p in range(pieces):
            for d in range(1, fast):
                side_copy(t, d, p).wait()
            value = kept[t, rows(p)]
            for d in range(1, fast):
                value = value + held[n // 2 + d * slow + t, rows(p)].astype(F32)

            if t == slow - 1:
                out[rows(p)] = value
                continue
            kept[t, rows(p)] = value

            @pl.when(a > s)
            def _():
                @pl.when(s > 0)
                def _():
                    up_copy(a, p).wait_recv()
                    line_out[a, rows(p)] = kept[t, rows(p)] + line_in[a, rows(p)]

                @pl.when(s == 0)
                def _():
                    line_out[a, rows(p)] = kept[t, rows(p)]

                up_copy(a, p).start()

            @pl.when(a < s)
            def _():
                @pl.when(s < slow - 1)
                def _():
                    down_copy(a, p).wait_recv()
                    line_out[a, rows(p)] = kept[t, rows(p)] + line_in[a, rows(p)]

                @pl.when(s == slow - 1)
                def _():
                    line_out[a, rows(p)] = kept[t, rows(p)]

                down_copy(a, p).start()

    def settle(i):
        middle(*order[i])
        t, d = order[i]
        if d == 0 and t > 0:
            finish(t - 1)

    for i, pair in enumerate(order):
        begin(*pair)
        if i:
            settle(i - 1)
    settle(len(order) - 1)
    finish(slow - 1)

    for p in range(pieces):

        @pl.when(s > 0)
        def _():
            up_copy(s, p).wait_recv()
            out[rows(p)] += line_in[s, rows(p)]

        @pl.when(s < slow - 1)
        def _():
            down_copy(s, p).wait_recv()
            out[rows(p)] += line_in[slow, rows(p)]

    for t in range(slow - 1):
        a = owners[t]
        for p in range(pieces):
            pl.when(a > s)(lambda: up_copy(a, p).wait_send())
            pl.when(a < s)(lambda: down_copy(a, p).wait_send())


def kernel(
    n, pieces, scale, traces, mine, basis, out,
    data, sketched, gram, weights,
    held, acc, own, pair_in, pair_sum, quick_in, line_in,
    up_send, down_send, side_send, core_send, recv,
    g_send, g_recv, *project_scratch,
):
    slow, fast = plan(n)
    me, s, f, c = place(fast)
    half = sketched.shape[1]

    def index(a, b, e):
        return (a * fast + b) * 2 + e

    partner = index(s, f, 1 - c)
    sides = [index(s, (f + d) % fast, c) for d in range(1, fast)]
    lines = [index((s + d) % slow, f, c) for d in range(1, slow)]
    greet([partner] + sides + lines)

    def block(slot, first):
        return mine if first else held.at[slot]

    def to_up(slot, first=False):
        return remote(block(slot, first), held.at[slot], up_send.at[slot], recv.at[slot], index(jnp.minimum(s + 1, slow - 1), f, c))

    def to_down(slot, first=False):
        return remote(block(slot, first), held.at[slot], down_send.at[slot], recv.at[slot], index(jnp.maximum(s - 1, 0), f, c))

    def to_side(d, slot, first=False):
        return remote(block(slot, first), held.at[slot], side_send.at[d, slot], recv.at[slot], sides[d])

    def to_core(slot, first=False):
        return remote(block(slot, first), held.at[slot], core_send.at[slot], recv.at[slot], partner)

    def arrived(slot):
        remote(held.at[slot], held.at[slot], core_send.at[slot], recv.at[slot], partner).wait_recv()

    def add(slot, first=False):
        value = mine[...] if first else held[slot]
        acc[...] += lax.dot_general(
            data[slot], value, (((1,), (1,)), ((), ())), preferred_element_type=F32
        )

    pl.when(s < slow - 1)(lambda: to_up(me, True).start())
    pl.when(s > 0)(lambda: to_down(me, True).start())
    for d in range(fast - 1):
        to_side(d, me, True).start()
    to_core(me, True).start()
    share = mine.shape[1]
    for j in range(n):
        data[j] = traces[:, j * share : (j + 1) * share]
    acc[...] = jnp.zeros_like(acc)
    add(me, True)

    for d in range(1, slow):

        @pl.when(s - d >= 0)
        def _(d=d):
            slot = index(s - d, f, c)
            arrived(slot)
            pl.when(s < slow - 1)(lambda: to_up(slot).start())
            for e in range(fast - 1):
                to_side(e, slot).start()
            to_core(slot).start()
            add(slot)

        @pl.when(s + d < slow)
        def _(d=d):
            slot = index(s + d, f, c)
            arrived(slot)
            pl.when(s > 0)(lambda: to_down(slot).start())
            for e in range(fast - 1):
                to_side(e, slot).start()
            to_core(slot).start()
            add(slot)

    def across(b):
        for d in range(slow):
            for sign in ((1,) if d == 0 else (-1, 1)):

                @pl.when((s + sign * d >= 0) & (s + sign * d < slow))
                def _(d=d, sign=sign):
                    slot = index(s + sign * d, b, c)
                    arrived(slot)
                    to_core(slot).start()
                    add(slot)

    for d in range(1, fast):
        across((f + d) % fast)

    def other(b):
        for d in range(slow):
            for sign in ((1,) if d == 0 else (-1, 1)):

                @pl.when((s + sign * d >= 0) & (s + sign * d < slow))
                def _(d=d, sign=sign):
                    slot = index(s + sign * d, b, 1 - c)
                    arrived(slot)
                    add(slot)

    for d in range(fast):
        other((f + d) % fast)

    to_core(me, True).wait_send()
    pl.when(s < slow - 1)(lambda: to_up(me, True).wait_send())
    pl.when(s > 0)(lambda: to_down(me, True).wait_send())
    for e in range(fast - 1):
        to_side(e, me, True).wait_send()
    for d in range(1, slow):

        @pl.when(s - d >= 0)
        def _(d=d):
            slot = index(s - d, f, c)
            pl.when(s < slow - 1)(lambda: to_up(slot).wait_send())
            for e in range(fast - 1):
                to_side(e, slot).wait_send()
            to_core(slot).wait_send()

        @pl.when(s + d < slow)
        def _(d=d):
            slot = index(s + d, f, c)
            pl.when(s > 0)(lambda: to_down(slot).wait_send())
            for e in range(fast - 1):
                to_side(e, slot).wait_send()
            to_core(slot).wait_send()

    for d in range(1, fast):
        for a in range(slow):
            to_core(index(a, (f + d) % fast, c)).wait_send()

    rows = half
    width = sketched.shape[2]
    re = acc[:rows, :width] - acc[rows:, width:]
    im = acc[:rows, width:] + acc[rows:, :width]
    sketched[0] = re
    sketched[1] = im
    first = ((0,), (0,))
    gram_re = exact(re, re, first) + exact(im, im, first)
    gram_im = exact(re, im, first) - exact(im, re, first)
    row = lax.broadcasted_iota(jnp.int32, gram_re.shape, 0)
    col = lax.broadcasted_iota(jnp.int32, gram_re.shape, 1)
    own[...] = jnp.where(col >= row, gram_re, gram_im)

    step = remote(own, pair_in, g_send.at[0], g_recv.at[0], partner)
    step.start()
    step.wait()
    pair_sum[...] = own[...] + pair_in[...]
    steps = [
        remote(pair_sum, quick_in.at[d], g_send.at[1 + d], g_recv.at[1 + d], sides[d])
        for d in range(fast - 1)
    ]
    for step in steps:
        step.start()
    for step in steps:
        step.wait()
    total = pair_sum[...]
    for d in range(fast - 1):
        total = total + quick_in[d]
    line_in[s] = total
    steps = [
        remote(line_in.at[s], line_in.at[s], g_send.at[fast + d], g_recv.at[fast + d], lines[d])
        for d in range(slow - 1)
    ]
    for step in steps:
        step.start()
    for d in range(slow - 1):
        steps[d].wait()
    total = line_in[0]
    for a in range(1, slow):
        total = total + line_in[a]
    gram[...] = total
    factor(scale, gram, sketched, basis, weights)
    project(n, pieces, data, weights, out, held, *project_scratch)


def per_device(n, traces, sketch):
    slow, fast = plan(n)
    parts, rows, sources = traces.shape
    width, share = sketch.shape[1], sketch.shape[2]
    dma = pltpu.SemaphoreType.DMA
    vmem = pl.BlockSpec(memory_space=VMEM)
    two = 2 * width
    chunk = (two, share)
    pieces = 4 if n <= 64 and two % 64 == 0 else 1
    scale = math.sqrt(rows * n)
    square = (width, width)
    basis, coeffs = pl.pallas_call(
        functools.partial(kernel, n, pieces, scale),
        out_shape=(
            jax.ShapeDtypeStruct((2, rows, width), F32),
            jax.ShapeDtypeStruct(chunk, F32),
        ),
        in_specs=[vmem] * 2,
        out_specs=(vmem, vmem),
        scratch_shapes=[
            VMEM((n, 2 * rows, share), BF16),
            VMEM((2, rows, width), F32),
            VMEM(square, F32),
            VMEM((two, 2 * rows), BF16),
            VMEM((n, two, share), BF16),
            VMEM((2 * rows, two), F32),
            VMEM(square, F32),
            VMEM(square, F32),
            VMEM(square, F32),
            VMEM((max(fast - 1, 1),) + square, F32),
            VMEM((slow,) + square, F32),
            dma((n,)),
            dma((n,)),
            dma((max(fast - 1, 1), n)),
            dma((n,)),
            dma((n,)),
            dma((slow + fast,)),
            dma((slow + fast,)),
            VMEM((slow,) + chunk, F32),
            VMEM(chunk, F32),
            VMEM((fast, slow) + chunk, F32),
            VMEM((fast, slow) + chunk, F32),
            VMEM((slow,) + chunk, F32),
            VMEM((slow + 1,) + chunk, F32),
        ]
        + [dma((fast, slow, pieces))] * 4
        + [dma((slow, pieces))] * 4,
        compiler_params=pltpu.CompilerParams(
            collective_id=0, has_side_effects=True, vmem_limit_bytes=LIMIT
        ),
        name="range_finder",
    )(traces.reshape(2 * rows, sources), sketch.reshape(two, share))
    return basis, coeffs.reshape(2, width, share)


def solution(mesh):
    return jax.shard_map(
        functools.partial(per_device, mesh.shape["rcv"]),
        mesh=mesh,
        in_specs=(P(None, ("grp", "rcv"), None), P(None, None, "rcv")),
        out_specs=(P(None, ("grp", "rcv"), None), P(None, "grp", "rcv")),
        check_vma=False,
    )
```

```python
import functools
import math

import jax
import jax.numpy as jnp
from jax import lax
from jax.experimental import pallas as pl
from jax.experimental.pallas import tpu as pltpu
from jax.sharding import PartitionSpec as P

VMEM = pltpu.VMEM
F32 = jnp.float32
BF16 = jnp.bfloat16
LIMIT = 67_000_000


def plan(n):
    chips = n // 2
    fast = max(d for d in range(1, chips + 1) if chips % d == 0 and d * d <= chips)
    return chips // fast, fast


def exact(left, right, dims):
    return lax.dot_general(
        left, right, (dims, ((), ())), precision=lax.Precision.HIGHEST, preferred_element_type=F32
    )


def remote(src, dst, send, recv, target):
    return pltpu.make_async_remote_copy(
        src_ref=src, dst_ref=dst, send_sem=send, recv_sem=recv,
        device_id={"rcv": target}, device_id_type=pl.DeviceIdType.MESH,
    )


def place(fast):
    me = lax.axis_index("rcv")
    chip = me // 2
    return me, chip // fast, chip % fast, me % 2


def greet(targets):
    barrier = pltpu.get_barrier_semaphore()
    for target in targets:
        pl.semaphore_signal(
            barrier, inc=1, device_id={"rcv": target}, device_id_type=pl.DeviceIdType.MESH
        )
    pl.semaphore_wait(barrier, len(targets))


def factor(scale, gram, sketched, basis, weights):
    packed = gram[...]
    width = packed.shape[0]
    turned = packed.T
    row = lax.broadcasted_iota(jnp.int32, packed.shape, 0)
    col = lax.broadcasted_iota(jnp.int32, packed.shape, 1)
    g_re = jnp.where(col >= row, packed, turned)
    g_im = jnp.where(row > col, packed, jnp.where(row < col, -turned, 0.0))
    tile = 8
    count = width // tile
    re = [g_re[tile * i : tile * (i + 1)] for i in range(count)]
    im = [g_im[tile * i : tile * (i + 1)] for i in range(count)]
    lane = lax.broadcasted_iota(jnp.int32, (tile, width), 1)
    sub = lax.broadcasted_iota(jnp.int32, (tile, width), 0)
    for k in range(width):
        at, inside = divmod(k, tile)
        d = re[at][inside : inside + 1, k : k + 1]
        here = lane[:1] == k
        p_re = jnp.where(here, 1.0, re[at][inside : inside + 1, :])
        p_im = jnp.where(here, 0.0, im[at][inside : inside + 1, :])
        inv = 1.0 / d
        q_re = p_re * inv
        q_im = p_im * inv
        for i in range(at, count):
            c_re = re[i][:, k : k + 1]
            c_im = im[i][:, k : k + 1]
            old_re = jnp.where(lane == k, 0.0, re[i])
            old_im = jnp.where(lane == k, 0.0, im[i])
            new_re = old_re - (c_re * q_re - c_im * q_im)
            new_im = old_im - (c_re * q_im + c_im * q_re)
            if i == at:
                root = lax.rsqrt(d)
                new_re = jnp.where(sub > inside, new_re, jnp.where(sub == inside, jnp.where(lane > k, 0.0, p_re * root), re[i]))
                new_im = jnp.where(sub > inside, new_im, jnp.where(sub == inside, jnp.where(lane > k, 0.0, p_im * root), im[i]))
            re[i] = new_re
            im[i] = new_im
    l_re = jnp.concatenate(re, axis=0)
    l_im = jnp.concatenate(im, axis=0)
    s_re, s_im = sketched[0], sketched[1]
    last = ((1,), (1,))
    o_re = exact(s_re, l_re, last) + exact(s_im, l_im, last)
    o_im = exact(s_im, l_re, last) - exact(s_re, l_im, last)
    basis[0] = o_re * scale
    basis[1] = o_im * scale
    t_re, t_im = o_re.T, o_im.T
    rows = o_re.shape[0]
    weights[:width, :rows] = t_re.astype(BF16)
    weights[:width, rows:] = t_im.astype(BF16)
    weights[width:, :rows] = (-t_im).astype(BF16)
    weights[width:, rows:] = t_re.astype(BF16)


def project(
    n, pieces, data, weights, out, held,
    kept, fresh, away, from_core, line_out, line_in, near_out, near_in,
    c_send, c_recv, s_send, s_recv, u_send, u_recv, d_send, d_recv, n_send, n_recv,
):
    slow, fast = plan(n)
    me, s, f, c = place(fast)
    depth = out.shape[0] // pieces

    def index(a, b, e):
        return (a * fast + b) * 2 + e

    partner = index(s, f, 1 - c)
    sides = [index(s, (f + d) % fast, c) for d in range(1, fast)]

    def rows(p):
        return pl.ds(p * depth, depth)

    def product(slot):
        return jnp.dot(weights[...], data[slot], preferred_element_type=F32)

    def core_copy(t, d, p):
        return remote(away.at[d, t, rows(p)], from_core.at[d, t, rows(p)], c_send.at[d, t, p], c_recv.at[d, t, p], partner)

    def side_copy(t, d, p):
        return remote(held.at[d * slow + t, rows(p)], held.at[n // 2 + d * slow + t, rows(p)], s_send.at[d, t, p], s_recv.at[d, t, p], sides[d - 1])

    orders = [
        sorted(range(slow), key=lambda a: (-abs(a - b), -a if 2 * b < slow else a)) for b in range(slow)
    ]

    def target(t):
        value = 0
        for b in range(slow):
            value = value + jnp.where(s == b, orders[b][t], 0)
        return value

    owners = [target(t) for t in range(slow)]

    def begin(t, d):
        a, b = owners[t], (f + d) % fast
        away[d, t] = product(index(a, b, 1 - c))
        for p in range(pieces):
            core_copy(t, d, p).start()

    def middle(t, d):
        into = kept.at[t] if d == 0 else fresh
        into[...] = product(index(owners[t], (f + d) % fast, c))
        for p in range(pieces):
            core_copy(t, d, p).wait()
            value = into[rows(p)] + from_core[d, t, rows(p)]
            if d == 0:
                kept[t, rows(p)] = value
            else:
                held[d * slow + t, rows(p)] = value.astype(BF16)
                side_copy(t, d, p).start()

    order = [(t, d) for t in range(slow) for d in list(range(1, fast)) + [0]]

    def up_copy(a, p):
        return remote(line_out.at[a, rows(p)], line_in.at[a, rows(p)], u_send.at[a, p], u_recv.at[a, p], index(jnp.minimum(s + 1, slow - 1), f, c))

    def down_copy(a, p):
        slot = jnp.where(a == s - 1, slow, a)
        return remote(line_out.at[a, rows(p)], line_in.at[slot, rows(p)], d_send.at[a, p], d_recv.at[a, p], index(jnp.maximum(s - 1, 0), f, c))

    def near_copy(k, p):
        goal = index(min(1, slow - 1) if k == 0 else max(slow - 2, 0), f, c)
        return remote(near_out.at[rows(p)], near_in.at[k, rows(p)], n_send.at[p], n_recv.at[k, p], goal)

    def near_up(a):
        return (s == 0) & (a == 1)

    def near_down(a):
        return (s == slow - 1) & (a == slow - 2)

    def finish(t):
        a = owners[t]
        for p in range(pieces):
            for d in range(1, fast):
                side_copy(t, d, p).wait()
            value = kept[t, rows(p)]
            for d in range(1, fast):
                value = value + held[n // 2 + d * slow + t, rows(p)].astype(F32)

            if t == slow - 1:
                out[rows(p)] = value
                continue
            kept[t, rows(p)] = value

            @pl.when(near_up(a))
            def _():
                near_out[rows(p)] = value.astype(BF16)
                near_copy(0, p).start()

            @pl.when(near_down(a))
            def _():
                near_out[rows(p)] = value.astype(BF16)
                near_copy(1, p).start()

            @pl.when((a > s) & jnp.logical_not(near_up(a)))
            def _():
                @pl.when(s > 0)
                def _():
                    up_copy(a, p).wait_recv()
                    line_out[a, rows(p)] = kept[t, rows(p)] + line_in[a, rows(p)]

                @pl.when(s == 0)
                def _():
                    line_out[a, rows(p)] = kept[t, rows(p)]

                up_copy(a, p).start()

            @pl.when((a < s) & jnp.logical_not(near_down(a)))
            def _():
                @pl.when(s < slow - 1)
                def _():
                    down_copy(a, p).wait_recv()
                    line_out[a, rows(p)] = kept[t, rows(p)] + line_in[a, rows(p)]

                @pl.when(s == slow - 1)
                def _():
                    line_out[a, rows(p)] = kept[t, rows(p)]

                down_copy(a, p).start()

    def settle(i):
        middle(*order[i])
        t, d = order[i]
        if d == 0 and t > 0:
            finish(t - 1)

    for i, pair in enumerate(order):
        begin(*pair)
        if i:
            settle(i - 1)
    settle(len(order) - 1)
    finish(slow - 1)

    for p in range(pieces):

        @pl.when(s == 1)
        def _():
            near_copy(0, p).wait_recv()
            out[rows(p)] += near_in[0, rows(p)].astype(F32)

        @pl.when(s == slow - 2)
        def _():
            near_copy(1, p).wait_recv()
            out[rows(p)] += near_in[1, rows(p)].astype(F32)

        @pl.when(s > 1)
        def _():
            up_copy(s, p).wait_recv()
            out[rows(p)] += line_in[s, rows(p)]

        @pl.when(s < slow - 2)
        def _():
            down_copy(s, p).wait_recv()
            out[rows(p)] += line_in[slow, rows(p)]

    for t in range(slow - 1):
        a = owners[t]
        for p in range(pieces):
            pl.when(near_up(a))(lambda: near_copy(0, p).wait_send())
            pl.when(near_down(a))(lambda: near_copy(1, p).wait_send())
            pl.when((a > s) & jnp.logical_not(near_up(a)))(lambda: up_copy(a, p).wait_send())
            pl.when((a < s) & jnp.logical_not(near_down(a)))(lambda: down_copy(a, p).wait_send())


def kernel(
    n, pieces, scale, traces, mine, basis, out,
    data, sketched, gram, weights,
    held, acc, own, pair_in, pair_sum, quick_in, line_in,
    up_send, down_send, side_send, core_send, recv,
    g_send, g_recv, *project_scratch,
):
    slow, fast = plan(n)
    me, s, f, c = place(fast)
    half = sketched.shape[1]

    def index(a, b, e):
        return (a * fast + b) * 2 + e

    partner = index(s, f, 1 - c)
    sides = [index(s, (f + d) % fast, c) for d in range(1, fast)]
    lines = [index((s + d) % slow, f, c) for d in range(1, slow)]
    greet([partner] + sides + lines)

    size = mine.shape[0] // pieces

    def piece(p):
        return pl.ds(p * size, size)

    def send(kind, slot, p, first, where):
        source = mine.at[piece(p)] if first else held.at[slot, piece(p)]
        return remote(source, held.at[slot, piece(p)], kind.at[slot, p], recv.at[slot, p], where)

    above = index(jnp.minimum(s + 1, slow - 1), f, c)
    below = index(jnp.maximum(s - 1, 0), f, c)

    def to_up(slot, p, first=False):
        return send(up_send, slot, p, first, above)

    def to_down(slot, p, first=False):
        return send(down_send, slot, p, first, below)

    def to_side(d, slot, p, first=False):
        return send(side_send.at[d], slot, p, first, sides[d])

    def to_core(slot, p, first=False):
        return send(core_send, slot, p, first, partner)

    def arrived(slot, p):
        to_core(slot, p).wait_recv()

    def add(slot, first=False):
        value = mine[...] if first else held[slot]
        acc[...] += lax.dot_general(
            data[slot], value, (((1,), (1,)), ((), ())), preferred_element_type=F32
        )

    def spread(act, slot, p, up, down, first=False):
        if up:
            pl.when(s < slow - 1)(lambda: act(to_up(slot, p, first)))
        if down:
            pl.when(s > 0)(lambda: act(to_down(slot, p, first)))
        for d in range(fast - 1):
            act(to_side(d, slot, p, first))
        act(to_core(slot, p, first))

    def begin(copy):
        copy.start()

    def sent(copy):
        copy.wait_send()

    for p in range(pieces):
        spread(begin, me, p, True, True, True)
    share = mine.shape[1]
    for j in range(n):
        data[j] = traces[:, j * share : (j + 1) * share]
    acc[...] = jnp.zeros_like(acc)
    add(me, True)

    for d in range(1, slow):
        for p in range(pieces):

            @pl.when(s - d >= 0)
            def _():
                arrived(index(s - d, f, c), p)
                spread(begin, index(s - d, f, c), p, True, False)

            @pl.when(s + d < slow)
            def _():
                arrived(index(s + d, f, c), p)
                spread(begin, index(s + d, f, c), p, False, True)

        pl.when(s - d >= 0)(lambda: add(index(s - d, f, c)))
        pl.when(s + d < slow)(lambda: add(index(s + d, f, c)))

    def remaining(b, e, pass_on):
        for d in range(slow):
            for sign in (1,) if d == 0 else (-1, 1):

                @pl.when((s + sign * d >= 0) & (s + sign * d < slow))
                def _():
                    slot = index(s + sign * d, b, e)
                    for p in range(pieces):
                        arrived(slot, p)
                        if pass_on:
                            to_core(slot, p).start()
                    add(slot)

    for d in range(1, fast):
        remaining((f + d) % fast, c, True)
    for d in range(fast):
        remaining((f + d) % fast, 1 - c, False)

    for p in range(pieces):
        spread(sent, me, p, True, True, True)
        for d in range(1, slow):
            pl.when(s - d >= 0)(lambda: spread(sent, index(s - d, f, c), p, True, False))
            pl.when(s + d < slow)(lambda: spread(sent, index(s + d, f, c), p, False, True))
        for d in range(1, fast):
            for a in range(slow):
                to_core(index(a, (f + d) % fast, c), p).wait_send()

    rows = half
    width = sketched.shape[2]
    re = acc[:rows, :width] - acc[rows:, width:]
    im = acc[:rows, width:] + acc[rows:, :width]
    sketched[0] = re
    sketched[1] = im
    first = ((0,), (0,))
    gram_re = exact(re, re, first) + exact(im, im, first)
    cross = exact(re, im, first)
    gram_im = cross - cross.T
    row = lax.broadcasted_iota(jnp.int32, gram_re.shape, 0)
    col = lax.broadcasted_iota(jnp.int32, gram_re.shape, 1)
    own[...] = jnp.where(col >= row, gram_re, gram_im)

    step = remote(own, pair_in, g_send.at[0], g_recv.at[0], partner)
    step.start()
    step.wait()
    pair_sum[...] = own[...] + pair_in[...]
    steps = [
        remote(pair_sum, quick_in.at[d], g_send.at[1 + d], g_recv.at[1 + d], sides[d])
        for d in range(fast - 1)
    ]
    for step in steps:
        step.start()
    for step in steps:
        step.wait()
    total = pair_sum[...]
    for d in range(fast - 1):
        total = total + quick_in[d]
    line_in[s] = total
    steps = [
        remote(line_in.at[s], line_in.at[s], g_send.at[fast + d], g_recv.at[fast + d], lines[d])
        for d in range(slow - 1)
    ]
    for step in steps:
        step.start()
    for d in range(slow - 1):
        steps[d].wait()
    total = line_in[0]
    for a in range(1, slow):
        total = total + line_in[a]
    gram[...] = total
    factor(scale, gram, sketched, basis, weights)
    project(n, pieces, data, weights, out, held, *project_scratch)


def per_device(n, traces, sketch):
    slow, fast = plan(n)
    parts, rows, sources = traces.shape
    width, share = sketch.shape[1], sketch.shape[2]
    dma = pltpu.SemaphoreType.DMA
    vmem = pl.BlockSpec(memory_space=VMEM)
    two = 2 * width
    chunk = (two, share)
    pieces = 4 if n <= 64 and two % 64 == 0 else 1
    scale = math.sqrt(rows * n)
    square = (width, width)
    basis, coeffs = pl.pallas_call(
        functools.partial(kernel, n, pieces, scale),
        out_shape=(
            jax.ShapeDtypeStruct((2, rows, width), F32),
            jax.ShapeDtypeStruct(chunk, F32),
        ),
        in_specs=[vmem] * 2,
        out_specs=(vmem, vmem),
        scratch_shapes=[
            VMEM((n, 2 * rows, share), BF16),
            VMEM((2, rows, width), F32),
            VMEM(square, F32),
            VMEM((two, 2 * rows), BF16),
            VMEM((n, two, share), BF16),
            VMEM((2 * rows, two), F32),
            VMEM(square, F32),
            VMEM(square, F32),
            VMEM(square, F32),
            VMEM((max(fast - 1, 1),) + square, F32),
            VMEM((slow,) + square, F32),
            dma((n, pieces)),
            dma((n, pieces)),
            dma((max(fast - 1, 1), n, pieces)),
            dma((n, pieces)),
            dma((n, pieces)),
            dma((slow + fast,)),
            dma((slow + fast,)),
            VMEM((slow,) + chunk, F32),
            VMEM(chunk, F32),
            VMEM((fast, slow) + chunk, F32),
            VMEM((fast, slow) + chunk, F32),
            VMEM((slow,) + chunk, F32),
            VMEM((slow + 1,) + chunk, F32),
            VMEM(chunk, BF16),
            VMEM((2,) + chunk, BF16),
        ]
        + [dma((fast, slow, pieces))] * 4
        + [dma((slow, pieces))] * 4
        + [dma((pieces,)), dma((2, pieces))],
        compiler_params=pltpu.CompilerParams(
            collective_id=0, has_side_effects=True, vmem_limit_bytes=LIMIT
        ),
        name="range_finder",
    )(traces.reshape(2 * rows, sources), sketch.reshape(two, share))
    return basis, coeffs.reshape(2, width, share)


def solution(mesh):
    return jax.shard_map(
        functools.partial(per_device, mesh.shape["rcv"]),
        mesh=mesh,
        in_specs=(P(None, ("grp", "rcv"), None), P(None, None, "rcv")),
        out_specs=(P(None, ("grp", "rcv"), None), P(None, "grp", "rcv")),
        check_vma=False,
    )
```

```python
import functools
import math

import jax
import jax.numpy as jnp
from jax import lax
from jax.experimental import pallas as pl
from jax.experimental.pallas import tpu as pltpu
from jax.sharding import PartitionSpec as P

VMEM = pltpu.VMEM
F32 = jnp.float32
BF16 = jnp.bfloat16
LIMIT = 67_000_000


def plan(n):
    chips = n // 2
    fast = max(d for d in range(1, chips + 1) if chips % d == 0 and d * d <= chips)
    return chips // fast, fast


def exact(left, right, dims):
    return lax.dot_general(
        left, right, (dims, ((), ())), precision=lax.Precision.HIGHEST, preferred_element_type=F32
    )


def remote(src, dst, send, recv, target):
    return pltpu.make_async_remote_copy(
        src_ref=src, dst_ref=dst, send_sem=send, recv_sem=recv,
        device_id={"rcv": target}, device_id_type=pl.DeviceIdType.MESH,
    )


def place(fast):
    me = lax.axis_index("rcv")
    chip = me // 2
    return me, chip // fast, chip % fast, me % 2


def greet(targets):
    barrier = pltpu.get_barrier_semaphore()
    for target in targets:
        pl.semaphore_signal(
            barrier, inc=1, device_id={"rcv": target}, device_id_type=pl.DeviceIdType.MESH
        )
    pl.semaphore_wait(barrier, len(targets))


def factor(scale, gram, sketched, basis, weights):
    packed = gram[...]
    width = packed.shape[0]
    turned = packed.T
    row = lax.broadcasted_iota(jnp.int32, packed.shape, 0)
    col = lax.broadcasted_iota(jnp.int32, packed.shape, 1)
    g_re = jnp.where(col >= row, packed, turned)
    g_im = jnp.where(row > col, packed, jnp.where(row < col, -turned, 0.0))
    tile = 8
    count = width // tile
    re = [g_re[tile * i : tile * (i + 1)] for i in range(count)]
    im = [g_im[tile * i : tile * (i + 1)] for i in range(count)]
    lane = lax.broadcasted_iota(jnp.int32, (tile, width), 1)
    sub = lax.broadcasted_iota(jnp.int32, (tile, width), 0)
    for k in range(width):
        at, inside = divmod(k, tile)
        d = re[at][inside : inside + 1, k : k + 1]
        here = lane[:1] == k
        p_re = jnp.where(here, 1.0, re[at][inside : inside + 1, :])
        p_im = jnp.where(here, 0.0, im[at][inside : inside + 1, :])
        inv = 1.0 / d
        q_re = p_re * inv
        q_im = p_im * inv
        for i in range(at, count):
            c_re = re[i][:, k : k + 1]
            c_im = im[i][:, k : k + 1]
            old_re = jnp.where(lane == k, 0.0, re[i])
            old_im = jnp.where(lane == k, 0.0, im[i])
            new_re = old_re - (c_re * q_re - c_im * q_im)
            new_im = old_im - (c_re * q_im + c_im * q_re)
            if i == at:
                root = lax.rsqrt(d)
                new_re = jnp.where(sub > inside, new_re, jnp.where(sub == inside, jnp.where(lane > k, 0.0, p_re * root), re[i]))
                new_im = jnp.where(sub > inside, new_im, jnp.where(sub == inside, jnp.where(lane > k, 0.0, p_im * root), im[i]))
            re[i] = new_re
            im[i] = new_im
    l_re = jnp.concatenate(re, axis=0)
    l_im = jnp.concatenate(im, axis=0)
    s_re, s_im = sketched[0], sketched[1]
    last = ((1,), (1,))
    o_re = exact(s_re, l_re, last) + exact(s_im, l_im, last)
    o_im = exact(s_im, l_re, last) - exact(s_re, l_im, last)
    basis[0] = o_re * scale
    basis[1] = o_im * scale
    t_re, t_im = o_re.T, o_im.T
    rows = o_re.shape[0]
    weights[:width, :rows] = t_re.astype(BF16)
    weights[:width, rows:] = t_im.astype(BF16)
    weights[width:, :rows] = (-t_im).astype(BF16)
    weights[width:, rows:] = t_re.astype(BF16)


def project(
    n, pieces, data, weights, out, held,
    kept, fresh, away, from_core, line_out, line_in, near_out, near_in,
    c_send, c_recv, s_send, s_recv, u_send, u_recv, d_send, d_recv, n_send, n_recv,
):
    slow, fast = plan(n)
    me, s, f, c = place(fast)
    depth = out.shape[0] // pieces

    def index(a, b, e):
        return (a * fast + b) * 2 + e

    partner = index(s, f, 1 - c)
    sides = [index(s, (f + d) % fast, c) for d in range(1, fast)]

    def rows(p):
        return pl.ds(p * depth, depth)

    def product(slot):
        return jnp.dot(weights[...], data[slot], preferred_element_type=F32)

    def core_copy(t, d, p):
        return remote(away.at[d, t, rows(p)], from_core.at[d, t, rows(p)], c_send.at[d, t, p], c_recv.at[d, t, p], partner)

    def side_copy(t, d, p):
        return remote(held.at[d * slow + t, rows(p)], held.at[n // 2 + d * slow + t, rows(p)], s_send.at[d, t, p], s_recv.at[d, t, p], sides[d - 1])

    orders = [
        sorted(range(slow), key=lambda a: (-abs(a - b), -a if 2 * b < slow else a)) for b in range(slow)
    ]

    def target(t):
        value = 0
        for b in range(slow):
            value = value + jnp.where(s == b, orders[b][t], 0)
        return value

    owners = [target(t) for t in range(slow)]

    def begin(t, d):
        a, b = owners[t], (f + d) % fast
        away[d, t] = product(index(a, b, 1 - c))
        for p in range(pieces):
            core_copy(t, d, p).start()

    def middle(t, d):
        into = kept.at[t] if d == 0 else fresh
        into[...] = product(index(owners[t], (f + d) % fast, c))
        for p in range(pieces):
            core_copy(t, d, p).wait()
            value = into[rows(p)] + from_core[d, t, rows(p)]
            if d == 0:
                kept[t, rows(p)] = value
            else:
                held[d * slow + t, rows(p)] = value.astype(BF16)
                side_copy(t, d, p).start()

    order = [(t, d) for t in range(slow) for d in list(range(1, fast)) + [0]]

    def up_copy(a, p):
        return remote(line_out.at[a, rows(p)], line_in.at[a, rows(p)], u_send.at[a, p], u_recv.at[a, p], index(jnp.minimum(s + 1, slow - 1), f, c))

    def down_copy(a, p):
        slot = jnp.where(a == s - 1, slow, a)
        return remote(line_out.at[a, rows(p)], line_in.at[slot, rows(p)], d_send.at[a, p], d_recv.at[a, p], index(jnp.maximum(s - 1, 0), f, c))

    def near_copy(k, p):
        goal = index(min(1, slow - 1) if k == 0 else max(slow - 2, 0), f, c)
        return remote(near_out.at[rows(p)], near_in.at[k, rows(p)], n_send.at[p], n_recv.at[k, p], goal)

    def near_up(a):
        return (s == 0) & (a == 1)

    def near_down(a):
        return (s == slow - 1) & (a == slow - 2)

    def finish(t):
        a = owners[t]
        for p in range(pieces):
            for d in range(1, fast):
                side_copy(t, d, p).wait()
            value = kept[t, rows(p)]
            for d in range(1, fast):
                value = value + held[n // 2 + d * slow + t, rows(p)].astype(F32)

            if t == slow - 1:
                out[rows(p)] = value
                continue
            kept[t, rows(p)] = value

            @pl.when(near_up(a))
            def _():
                near_out[rows(p)] = value.astype(BF16)
                near_copy(0, p).start()

            @pl.when(near_down(a))
            def _():
                near_out[rows(p)] = value.astype(BF16)
                near_copy(1, p).start()

            @pl.when((a > s) & jnp.logical_not(near_up(a)))
            def _():
                @pl.when(s > 0)
                def _():
                    up_copy(a, p).wait_recv()
                    line_out[a, rows(p)] = kept[t, rows(p)] + line_in[a, rows(p)]

                @pl.when(s == 0)
                def _():
                    line_out[a, rows(p)] = kept[t, rows(p)]

                up_copy(a, p).start()

            @pl.when((a < s) & jnp.logical_not(near_down(a)))
            def _():
                @pl.when(s < slow - 1)
                def _():
                    down_copy(a, p).wait_recv()
                    line_out[a, rows(p)] = kept[t, rows(p)] + line_in[a, rows(p)]

                @pl.when(s == slow - 1)
                def _():
                    line_out[a, rows(p)] = kept[t, rows(p)]

                down_copy(a, p).start()

    def settle(i):
        middle(*order[i])
        t, d = order[i]
        if d == 0 and t > 0:
            finish(t - 1)

    for i, pair in enumerate(order):
        begin(*pair)
        if i:
            settle(i - 1)
    settle(len(order) - 1)
    finish(slow - 1)

    for p in range(pieces):

        @pl.when(s == 1)
        def _():
            near_copy(0, p).wait_recv()
            out[rows(p)] += near_in[0, rows(p)].astype(F32)

        @pl.when(s == slow - 2)
        def _():
            near_copy(1, p).wait_recv()
            out[rows(p)] += near_in[1, rows(p)].astype(F32)

        @pl.when(s > 1)
        def _():
            up_copy(s, p).wait_recv()
            out[rows(p)] += line_in[s, rows(p)]

        @pl.when(s < slow - 2)
        def _():
            down_copy(s, p).wait_recv()
            out[rows(p)] += line_in[slow, rows(p)]

    for t in range(slow - 1):
        a = owners[t]
        for p in range(pieces):
            pl.when(near_up(a))(lambda: near_copy(0, p).wait_send())
            pl.when(near_down(a))(lambda: near_copy(1, p).wait_send())
            pl.when((a > s) & jnp.logical_not(near_up(a)))(lambda: up_copy(a, p).wait_send())
            pl.when((a < s) & jnp.logical_not(near_down(a)))(lambda: down_copy(a, p).wait_send())


def kernel(
    n, pieces, scale, traces, mine, basis, out,
    data, sketched, gram, weights,
    held, acc, own, pair_in, pair_sum, quick_in, line_in,
    up_send, down_send, side_send, core_send, recv,
    g_send, g_recv, *project_scratch,
):
    slow, fast = plan(n)
    me, s, f, c = place(fast)
    half = sketched.shape[1]

    def index(a, b, e):
        return (a * fast + b) * 2 + e

    partner = index(s, f, 1 - c)
    sides = [index(s, (f + d) % fast, c) for d in range(1, fast)]
    lines = [index((s + d) % slow, f, c) for d in range(1, slow)]
    greet([partner] + sides + lines)

    size = mine.shape[0] // pieces

    def piece(p):
        return pl.ds(p * size, size)

    def send(kind, slot, p, first, where):
        source = mine.at[piece(p)] if first else held.at[slot, piece(p)]
        return remote(source, held.at[slot, piece(p)], kind.at[slot, p], recv.at[slot, p], where)

    above = index(jnp.minimum(s + 1, slow - 1), f, c)
    below = index(jnp.maximum(s - 1, 0), f, c)

    def to_up(slot, p, first=False):
        return send(up_send, slot, p, first, above)

    def to_down(slot, p, first=False):
        return send(down_send, slot, p, first, below)

    def to_side(d, slot, p, first=False):
        return send(side_send.at[d], slot, p, first, sides[d])

    def to_core(slot, p, first=False):
        return send(core_send, slot, p, first, partner)

    def arrived(slot, p):
        to_core(slot, p).wait_recv()

    def add(slot, first=False):
        value = mine[...] if first else held[slot]
        acc[...] += lax.dot_general(
            data[slot], value, (((1,), (1,)), ((), ())), preferred_element_type=F32
        )

    def spread(act, slot, p, up, down, first=False):
        if up:
            pl.when(s < slow - 1)(lambda: act(to_up(slot, p, first)))
        if down:
            pl.when(s > 0)(lambda: act(to_down(slot, p, first)))
        for d in range(fast - 1):
            act(to_side(d, slot, p, first))
        act(to_core(slot, p, first))

    def begin(copy):
        copy.start()

    def sent(copy):
        copy.wait_send()

    for p in range(pieces):
        spread(begin, me, p, True, True, True)
    share = mine.shape[1]
    for j in range(n):
        data[j] = traces[:, j * share : (j + 1) * share]
    acc[...] = jnp.zeros_like(acc)
    add(me, True)

    for d in range(1, slow):
        for p in range(pieces):

            @pl.when(s - d >= 0)
            def _():
                arrived(index(s - d, f, c), p)
                spread(begin, index(s - d, f, c), p, True, False)

            @pl.when(s + d < slow)
            def _():
                arrived(index(s + d, f, c), p)
                spread(begin, index(s + d, f, c), p, False, True)

        pl.when(s - d >= 0)(lambda: add(index(s - d, f, c)))
        pl.when(s + d < slow)(lambda: add(index(s + d, f, c)))

    def remaining(b, e, pass_on):
        for d in range(slow):
            for sign in (1,) if d == 0 else (-1, 1):

                @pl.when((s + sign * d >= 0) & (s + sign * d < slow))
                def _():
                    slot = index(s + sign * d, b, e)
                    for p in range(pieces):
                        arrived(slot, p)
                        if pass_on:
                            to_core(slot, p).start()
                    add(slot)

    for d in range(1, fast):
        remaining((f + d) % fast, c, True)
    for d in range(fast):
        remaining((f + d) % fast, 1 - c, False)

    for p in range(pieces):
        spread(sent, me, p, True, True, True)
        for d in range(1, slow):
            pl.when(s - d >= 0)(lambda: spread(sent, index(s - d, f, c), p, True, False))
            pl.when(s + d < slow)(lambda: spread(sent, index(s + d, f, c), p, False, True))
        for d in range(1, fast):
            for a in range(slow):
                to_core(index(a, (f + d) % fast, c), p).wait_send()

    rows = half
    width = sketched.shape[2]
    re = acc[:rows, :width] - acc[rows:, width:]
    im = acc[:rows, width:] + acc[rows:, :width]
    sketched[0] = re
    sketched[1] = im
    first = ((0,), (0,))
    gram_re = exact(re, re, first) + exact(im, im, first)
    cross = exact(re, im, first)
    gram_im = cross - cross.T
    row = lax.broadcasted_iota(jnp.int32, gram_re.shape, 0)
    col = lax.broadcasted_iota(jnp.int32, gram_re.shape, 1)
    own[...] = jnp.where(col >= row, gram_re, gram_im)

    step = remote(own, pair_in, g_send.at[0], g_recv.at[0], partner)
    step.start()
    step.wait()
    pair_sum[...] = own[...] + pair_in[...]
    steps = [
        remote(pair_sum, quick_in.at[d], g_send.at[1 + d], g_recv.at[1 + d], sides[d])
        for d in range(fast - 1)
    ]
    for step in steps:
        step.start()
    for step in steps:
        step.wait()
    total = pair_sum[...]
    for d in range(fast - 1):
        total = total + quick_in[d]
    line_in[s] = total
    steps = [
        remote(line_in.at[s], line_in.at[s], g_send.at[fast + d], g_recv.at[fast + d], lines[d])
        for d in range(slow - 1)
    ]
    for step in steps:
        step.start()
    for d in range(slow - 1):
        steps[d].wait()
    total = line_in[0]
    for a in range(1, slow):
        total = total + line_in[a]
    gram[...] = total
    factor(scale, gram, sketched, basis, weights)
    project(n, pieces, data, weights, out, held, *project_scratch)


def per_device(n, traces, sketch):
    slow, fast = plan(n)
    parts, rows, sources = traces.shape
    width, share = sketch.shape[1], sketch.shape[2]
    dma = pltpu.SemaphoreType.DMA
    vmem = pl.BlockSpec(memory_space=VMEM)
    two = 2 * width
    chunk = (two, share)
    pieces = 2 if n <= 64 and two % 64 == 0 else 1
    scale = math.sqrt(rows * n)
    square = (width, width)
    basis, coeffs = pl.pallas_call(
        functools.partial(kernel, n, pieces, scale),
        out_shape=(
            jax.ShapeDtypeStruct((2, rows, width), F32),
            jax.ShapeDtypeStruct(chunk, F32),
        ),
        in_specs=[vmem] * 2,
        out_specs=(vmem, vmem),
        scratch_shapes=[
            VMEM((n, 2 * rows, share), BF16),
            VMEM((2, rows, width), F32),
            VMEM(square, F32),
            VMEM((two, 2 * rows), BF16),
            VMEM((n, two, share), BF16),
            VMEM((2 * rows, two), F32),
            VMEM(square, F32),
            VMEM(square, F32),
            VMEM(square, F32),
            VMEM((max(fast - 1, 1),) + square, F32),
            VMEM((slow,) + square, F32),
            dma((n, pieces)),
            dma((n, pieces)),
            dma((max(fast - 1, 1), n, pieces)),
            dma((n, pieces)),
            dma((n, pieces)),
            dma((slow + fast,)),
            dma((slow + fast,)),
            VMEM((slow,) + chunk, F32),
            VMEM(chunk, F32),
            VMEM((fast, slow) + chunk, F32),
            VMEM((fast, slow) + chunk, F32),
            VMEM((slow,) + chunk, F32),
            VMEM((slow + 1,) + chunk, F32),
            VMEM(chunk, BF16),
            VMEM((2,) + chunk, BF16),
        ]
        + [dma((fast, slow, pieces))] * 4
        + [dma((slow, pieces))] * 4
        + [dma((pieces,)), dma((2, pieces))],
        compiler_params=pltpu.CompilerParams(
            collective_id=0, has_side_effects=True, vmem_limit_bytes=LIMIT
        ),
        name="range_finder",
    )(traces.reshape(2 * rows, sources), sketch.reshape(two, share))
    return basis, coeffs.reshape(2, width, share)


def solution(mesh):
    return jax.shard_map(
        functools.partial(per_device, mesh.shape["rcv"]),
        mesh=mesh,
        in_specs=(P(None, ("grp", "rcv"), None), P(None, None, "rcv")),
        out_specs=(P(None, ("grp", "rcv"), None), P(None, "grp", "rcv")),
        check_vma=False,
    )
```
